256 devices in a mesh: head: 4 (over x_hi, core), blk: 64 (over z, x_lo, y).
Axes of the slice: x: 4 (x_hi: 2, x_lo: 2; x = x_hi * 2 + x_lo), y: 4, z: 8, core: 2. Of those that a mesh axis runs over, the one named last changes fastest.
Arguments:
- query: bfloat16 [32768, 8192], P(('blk', 'head'))
- key: bfloat16 [32768, 1024], P(('blk', 'head'))
- value: bfloat16 [32768, 1024], P(('blk', 'head')), may hold values from -6 to 6
- output_gradient: bfloat16 [32768, 8192], P(('blk', 'head')), may hold values from -6 to 6
- pair_codes: int32 [64, 8, 8], P('blk'), may hold values from 0 to 15
- pair_counts: int32 [64, 8], P('blk'), may hold values from 1 to 8
Outputs:
- attn_out: bfloat16 [32768, 8192], P(('blk', 'head'))
- grad_query: bfloat16 [32768, 8192], P(('blk', 'head'))
- key_gradient: bfloat16 [32768, 1024], P(('blk', 'head'))
- value_gradient: bfloat16 [32768, 1024], P(('blk', 'head'))
The draws below stay inside these ranges and needn't reach their ends.
All inputs are finite; a program needn't handle non-finite values.
Results may differ from the reference program's by a relative error of at most 0.015.
Values may be sent and summed in bfloat16 or wider, within the bound.
No kernel may reach another device: no remote copies, remote signals or barrier semaphores. Data moves between devices by JAX's collectives and lax.ppermute only.
A program may use at most 128 MiB of HBM per device.

```python
import jax
import jax.numpy as jnp
import numpy as np
from jax import lax

QUERY_HEADS = 64
KEY_VALUE_HEADS = 8
HEAD_SIZE = 128
BLOCK = 128
NSTEP = 8
NB = 4
CAP = 8
SEQUENCE_TOKENS = 32768
N_BLK = 64


def drawn(key):
    base = jax.random.fold_in(key, 11)
    key_query, random_key_streams = jax.random.split(base, 2)
    queries = jnp.clip(jax.random.normal(key_query, (SEQUENCE_TOKENS, QUERY_HEADS * HEAD_SIZE), jnp.float32), -4.0, 4.0)
    key_tensor = jnp.clip(jax.random.normal(random_key_streams, (SEQUENCE_TOKENS, KEY_VALUE_HEADS * HEAD_SIZE), jnp.float32), -4.0, 4.0)
    return (queries, key_tensor)


def draw_query(key, part):
    return drawn(key)[0].astype(jnp.bfloat16)


def draw_key(key, part):
    return drawn(key)[1].astype(jnp.bfloat16)


def pattern(key):
    base = jax.random.fold_in(key, 29)
    key_level, key_extra, key_star, key_perm, key_lower = jax.random.split(base, 5)
    level = jax.random.randint(key_level, (N_BLK,), 1, 4)
    extra = jax.random.randint(key_extra, (N_BLK, NSTEP), 1, 5)
    steps_at = jnp.arange(NSTEP, dtype=jnp.int32)[None, :]
    groups_at = jnp.arange(N_BLK, dtype=jnp.int32)[:, None]
    counts = jnp.minimum(jnp.minimum(extra, 2 * level[:, None]), CAP)
    counts = jnp.where(steps_at == 0, NB + jnp.minimum(extra, level[:, None]), counts)
    star = jax.random.randint(key_star, (), 1, N_BLK)
    forced = jnp.logical_and(groups_at == star, steps_at == 1)
    counts = jnp.where(forced, CAP, counts)
    perm_keys = jax.random.split(key_perm, N_BLK * NSTEP)
    perms = jax.vmap(lambda single: jax.random.permutation(single, NB * NB))(perm_keys)
    codes = perms[:, :CAP].reshape(N_BLK, NSTEP, CAP).astype(jnp.int32)
    lower_table = np.array([row * NB + col for row in range(NB) for col in range(row)], dtype=np.int32)
    lower_keys = jax.random.split(key_lower, N_BLK)
    lower_perm = jax.vmap(lambda single: jax.random.permutation(single, lower_table.shape[0]))(lower_keys)
    lower_codes = jnp.asarray(lower_table)[lower_perm[:, :CAP - NB]]
    diagonal = jnp.broadcast_to(jnp.arange(NB, dtype=jnp.int32) * (NB + 1), (N_BLK, NB))
    first = jnp.concatenate([diagonal, lower_codes.astype(jnp.int32)], axis=1)
    codes = codes.at[:, 0, :].set(first)
    descending = (NB * NB - 1 - jnp.arange(CAP, dtype=jnp.int32))[None, None, :]
    codes = jnp.where(forced[:, :, None], descending, codes)
    return (codes.astype(jnp.int32), counts.astype(jnp.int32))


def draw_pair_codes(key, part):
    return pattern(key)[0]


def draw_pair_counts(key, part):
    return pattern(key)[1]


def steps_of(stream_key, extent, cuts, least, top_value):
    def one(axis_at, blocks):
        draws = jax.random.uniform(jax.random.fold_in(jax.random.fold_in(stream_key, 6), axis_at), (blocks,), jnp.float32, least / len(cuts), top_value / len(cuts))
        return jnp.repeat(jnp.exp(draws), extent[axis_at] // blocks).reshape((-1,) + (1,) * (len(extent) - axis_at - 1))

    loudness = one(*cuts[0])
    for cut in cuts[1:]:
        loudness = loudness * one(*cut)
    return loudness


def normal_values(key, shape, deviation, bound, cuts=(), held_as=jnp.bfloat16):
    loudness = steps_of(key, shape, cuts, -0.22, 0.18) if cuts else 1.0
    entries = jax.random.normal(key, shape, jnp.float32) * deviation * loudness
    return jnp.minimum(jnp.maximum(entries, -bound), bound).astype(held_as)


def setup_inputs(seed: int = 0) -> dict:
    splits = jax.random.split(jax.random.key(seed), 7)
    return {
        "query": draw_query(jax.random.fold_in(splits[6], 71), 0),
        "key": draw_key(jax.random.fold_in(splits[6], 71), 0),
        "value": normal_values(splits[2], (SEQUENCE_TOKENS, KEY_VALUE_HEADS * HEAD_SIZE), 1.0, 6.0, ((0, 256),)),
        "output_gradient": normal_values(splits[3], (SEQUENCE_TOKENS, QUERY_HEADS * HEAD_SIZE), 1.0, 6.0, ((0, 256),)),
        "pair_codes": draw_pair_codes(jax.random.fold_in(splits[6], 71), 0),
        "pair_counts": draw_pair_counts(jax.random.fold_in(splits[6], 71), 0),
    }


NEGATIVE_FILL = -1e30


def block_scores(q_blk, k_blk, query_block, key_block, first_step, score_scale):
    scores = jnp.einsum("qhgd,khd->hgqk", q_blk.astype(jnp.float32), k_blk.astype(jnp.float32)) * score_scale
    if first_step:
        rows_at = lax.broadcasted_iota(jnp.int32, scores.shape, 2)
        cols_at = lax.broadcasted_iota(jnp.int32, scores.shape, 3)
        allowed = jnp.logical_or(key_block != query_block, cols_at <= rows_at)
        scores = jnp.where(allowed, scores, NEGATIVE_FILL)
    return scores


def forward_pairs(loop_state, queries, key_tensor, values, codes, count, first_step, score_scale):
    def visit(index, carry):
        best, total, acc = carry
        code = codes[index]
        query_block = code // NB
        key_block = code % NB
        q_blk = lax.dynamic_slice_in_dim(queries, query_block * BLOCK, BLOCK, 0)
        k_blk = lax.dynamic_slice_in_dim(key_tensor, key_block * BLOCK, BLOCK, 0)
        v_blk = lax.dynamic_slice_in_dim(values, key_block * BLOCK, BLOCK, 0)
        scores = block_scores(q_blk, k_blk, query_block, key_block, first_step, score_scale)
        best_old = lax.dynamic_slice_in_dim(best, query_block * BLOCK, BLOCK, 2)
        total_old = lax.dynamic_slice_in_dim(total, query_block * BLOCK, BLOCK, 2)
        acc_old = lax.dynamic_slice_in_dim(acc, query_block * BLOCK, BLOCK, 0)
        best_new = jnp.maximum(best_old, jnp.max(scores, axis=-1))
        factor = jnp.exp(best_old - best_new)
        weights = jnp.exp(scores - best_new[..., None])
        total_new = factor * total_old + jnp.sum(weights, axis=-1)
        low = weights.astype(jnp.bfloat16).astype(jnp.float32)
        mixed = jnp.einsum("hgqk,khd->qhgd", low, v_blk.astype(jnp.float32))
        acc_new = jnp.transpose(factor, (2, 0, 1))[..., None] * acc_old + mixed
        best = lax.dynamic_update_slice_in_dim(best, best_new, query_block * BLOCK, 2)
        total = lax.dynamic_update_slice_in_dim(total, total_new, query_block * BLOCK, 2)
        acc = lax.dynamic_update_slice_in_dim(acc, acc_new, query_block * BLOCK, 0)
        return best, total, acc

    return lax.fori_loop(0, count, visit, loop_state)


def backward_pairs(loop_state, queries, grads, key_tensor, values, log_total, row_dot, codes, count, first_step, score_scale):
    def visit(index, carry):
        query_gradient, key_grad, value_grad = carry
        code = codes[index]
        query_block = code // NB
        key_block = code % NB
        q_blk = lax.dynamic_slice_in_dim(queries, query_block * BLOCK, BLOCK, 0)
        g_blk = lax.dynamic_slice_in_dim(grads, query_block * BLOCK, BLOCK, 0).astype(jnp.float32)
        k_blk = lax.dynamic_slice_in_dim(key_tensor, key_block * BLOCK, BLOCK, 0)
        v_blk = lax.dynamic_slice_in_dim(values, key_block * BLOCK, BLOCK, 0).astype(jnp.float32)
        scores = block_scores(q_blk, k_blk, query_block, key_block, first_step, score_scale)
        lse_blk = lax.dynamic_slice_in_dim(log_total, query_block * BLOCK, BLOCK, 2)
        row_blk = lax.dynamic_slice_in_dim(row_dot, query_block * BLOCK, BLOCK, 2)
        prob = jnp.exp(scores - lse_blk[..., None])
        low = prob.astype(jnp.bfloat16).astype(jnp.float32)
        value_part = jnp.einsum("hgqk,qhgd->khd", low, g_blk)
        dprob = jnp.einsum("qhgd,khd->hgqk", g_blk, v_blk)
        dscore = (prob * (dprob - row_blk[..., None])).astype(jnp.bfloat16).astype(jnp.float32)
        query_part = jnp.einsum("hgqk,khd->qhgd", dscore, k_blk.astype(jnp.float32))
        key_part = jnp.einsum("hgqk,qhgd->khd", dscore, q_blk.astype(jnp.float32))
        old_query = lax.dynamic_slice_in_dim(query_gradient, query_block * BLOCK, BLOCK, 0)
        query_gradient = lax.dynamic_update_slice_in_dim(query_gradient, old_query + query_part, query_block * BLOCK, 0)
        old_key = lax.dynamic_slice_in_dim(key_grad, key_block * BLOCK, BLOCK, 0)
        key_grad = lax.dynamic_update_slice_in_dim(key_grad, old_key + key_part, key_block * BLOCK, 0)
        old_value = lax.dynamic_slice_in_dim(value_grad, key_block * BLOCK, BLOCK, 0)
        value_grad = lax.dynamic_update_slice_in_dim(value_grad, old_value + value_part, key_block * BLOCK, 0)
        return query_gradient, key_grad, value_grad

    return lax.fori_loop(0, count, visit, loop_state)


def reference(query, key, value, output_gradient, pair_codes, pair_counts):
    device_sharding = QUERY_HEADS // KEY_VALUE_HEADS
    row_count_local = NB * BLOCK
    score_scale = HEAD_SIZE ** -0.5
    gathered_queries = query.reshape(N_BLK, row_count_local, KEY_VALUE_HEADS, device_sharding, HEAD_SIZE)
    gathered_gradients = output_gradient.reshape(N_BLK, row_count_local, KEY_VALUE_HEADS, device_sharding, HEAD_SIZE)
    gathered_keys = key.reshape(N_BLK, row_count_local, KEY_VALUE_HEADS, HEAD_SIZE)
    gathered_values = value.reshape(N_BLK, row_count_local, KEY_VALUE_HEADS, HEAD_SIZE)
    steps_range = jnp.arange(NSTEP, dtype=jnp.int32)

    def one_group(carry, inputs):
        key_gradient_sum, value_gradient_sum = carry
        queries, grads, codes, counts, group = inputs
        window = (group - steps_range) % N_BLK
        loop_state = (jnp.full((KEY_VALUE_HEADS, device_sharding, row_count_local), NEGATIVE_FILL, jnp.float32),
                 jnp.zeros((KEY_VALUE_HEADS, device_sharding, row_count_local), jnp.float32),
                 jnp.zeros((row_count_local, KEY_VALUE_HEADS, device_sharding, HEAD_SIZE), jnp.float32))
        for step in range(NSTEP):
            loop_state = forward_pairs(loop_state, queries, gathered_keys[window[step]], gathered_values[window[step]],
                                  codes[step], counts[step], step == 0, score_scale)
        best, total, acc = loop_state
        attn = (acc / jnp.transpose(total, (2, 0, 1))[..., None]).astype(jnp.bfloat16)
        log_total = best + jnp.log(total)
        row_dot = jnp.einsum("qhgd,qhgd->hgq", grads.astype(jnp.float32), attn.astype(jnp.float32))
        query_gradient = jnp.zeros((row_count_local, KEY_VALUE_HEADS, device_sharding, HEAD_SIZE), jnp.float32)
        for step in range(NSTEP):
            empty_key_value = jnp.zeros((row_count_local, KEY_VALUE_HEADS, HEAD_SIZE), jnp.float32)
            query_gradient, key_part, value_part = backward_pairs(
                (query_gradient, empty_key_value, empty_key_value), queries, grads, gathered_keys[window[step]],
                gathered_values[window[step]], log_total, row_dot, codes[step], counts[step], step == 0, score_scale)
            key_gradient_sum = key_gradient_sum.at[window[step]].add(key_part)
            value_gradient_sum = value_gradient_sum.at[window[step]].add(value_part)
        query_out = (query_gradient * score_scale).astype(jnp.bfloat16)
        return (key_gradient_sum, value_gradient_sum), (attn, query_out)

    start_offset = (jnp.zeros((N_BLK, row_count_local, KEY_VALUE_HEADS, HEAD_SIZE), jnp.float32), jnp.zeros((N_BLK, row_count_local, KEY_VALUE_HEADS, HEAD_SIZE), jnp.float32))
    groups = jnp.arange(N_BLK, dtype=jnp.int32)
    (key_gradient_sum, value_gradient_sum), (attn, query_out) = lax.scan(
        one_group, start_offset, (gathered_queries, gathered_gradients, pair_codes, pair_counts, groups))
    attn_out = attn.reshape(SEQUENCE_TOKENS, QUERY_HEADS * HEAD_SIZE)
    grad_query = query_out.reshape(SEQUENCE_TOKENS, QUERY_HEADS * HEAD_SIZE)
    key_gradient = (key_gradient_sum * score_scale).astype(jnp.bfloat16).reshape(SEQUENCE_TOKENS, KEY_VALUE_HEADS * HEAD_SIZE)
    value_gradient = value_gradient_sum.astype(jnp.bfloat16).reshape(SEQUENCE_TOKENS, KEY_VALUE_HEADS * HEAD_SIZE)
    return (attn_out, grad_query, key_gradient, value_gradient)
```

```python
import functools

import jax
import jax.numpy as jnp
from jax import lax
from jax.experimental import pallas as pl
from jax.experimental.pallas import tpu as pltpu
from jax.sharding import PartitionSpec as P

QUERY_HEADS = 64
KEY_VALUE_HEADS = 8
HEAD_SIZE = 128
BLOCK = 128
NSTEP = 8
NB = 4
QUAD = 4
GROUP = QUERY_HEADS // KEY_VALUE_HEADS
WIDE = GROUP * BLOCK
MOST = NSTEP * NB
NEGATIVE_FILL = -1e30
SCALE = HEAD_SIZE ** (-0.5)
SCALE_LOG2 = SCALE * 1.4426950408889634
TILE = 256
F32 = jnp.float32
BF16 = jnp.bfloat16

OWN, PREV = 0, 1
NEAR = {1: 2, 2: 4, 3: 3}
FAR = {1: 5, 2: 7, 3: 6}


def dot(a, b):
    return lax.dot_general(a, b, (((1,), (0,)), ((), ())), preferred_element_type=F32)


def attend(codes, counts, place, qd_ref, *refs):
    kv_refs = refs[:NSTEP]
    out_ref, own_ref = refs[NSTEP], refs[NSTEP + 1]
    part_refs = refs[NSTEP + 2 : 2 * NSTEP + 1]
    (
        pairs, filled, kvs, dkv, masks, q_t, q_s, g_t, g_s, scores, weights, top, total, row, turned, dsc,
    ) = refs[2 * NSTEP + 1 :]
    t = pl.program_id(0)

    @pl.when(t == 0)
    def _():
        y = place[0]
        for b in range(NB):
            pairs[b, 0] = b
            filled[b] = 1
        for s in range(NSTEP):
            d = s % QUAD
            if d == 0:
                slot = OWN if s == 0 else PREV
            elif s < QUAD:
                slot = jnp.where(y >= d, FAR[d], NEAR[d])
            else:
                slot = jnp.where(y >= d, NEAR[d], FAR[d])

            def add(i, carry, s=s, slot=slot):
                code = codes[s, i]
                b = lax.shift_right_logical(code, 2)
                c = jnp.bitwise_and(code, 3)

                def put():
                    n = filled[b]
                    pairs[b, n] = slot * NB + c
                    filled[b] = n + 1

                if s == 0:
                    pl.when(b != c)(put)
                else:
                    put()
                return carry

            lax.fori_loop(0, counts[s], add, 0)
        for b in range(NB):
            pairs[b, filled[b]] = b
        for s in range(NSTEP):
            for c in range(NB):
                kvs[s * NB + c] = kv_refs[s][pl.ds(c * BLOCK, BLOCK), :]
        dkv[...] = jnp.zeros_like(dkv)
        keys_at = lax.broadcasted_iota(jnp.int32, (BLOCK, BLOCK), 0)
        rows_at = lax.broadcasted_iota(jnp.int32, (BLOCK, BLOCK), 1)
        masks[0] = jnp.zeros((BLOCK, BLOCK), F32)
        masks[1] = jnp.where(keys_at <= rows_at, 0.0, NEGATIVE_FILL)
        masks[2] = jnp.full((BLOCK, BLOCK), NEGATIVE_FILL, F32)

    for h in range(GROUP):
        at = pl.ds(h * BLOCK, BLOCK)
        q = qd_ref[0, :, at]
        q_s[at, :] = q
        q_t[:, at] = q.T
        g_t[:, at] = qd_ref[1, :, at].T

    n = filled[t]
    trips = lax.shift_right_logical(n + 1, 1)
    top[...] = jnp.full_like(top, NEGATIVE_FILL)
    total[...] = jnp.zeros_like(total)
    turned[...] = jnp.zeros_like(turned)

    def two(i, lo):
        a, b = pairs[t, 2 * i], pairs[t, 2 * i + 1]
        return jnp.concatenate([kvs[a, :, pl.ds(lo, HEAD_SIZE)], kvs[b, :, pl.ds(lo, HEAD_SIZE)]], axis=0)

    def score_visit(i, carry):
        k = two(i, 0)
        first = masks[jnp.where(i == 0, 1, 0)]
        second = masks[jnp.where(2 * i + 1 >= n, 2, 0)]
        mask = jnp.concatenate([first, second], axis=0)
        mask = jnp.concatenate([mask, mask], axis=1)
        for w in range(WIDE // TILE):
            at = pl.ds(w * TILE, TILE)
            s = dot(k, q_t[:, at]) * SCALE_LOG2 + mask
            scores[pl.ds(2 * i, 2), :, at] = s.reshape(2, BLOCK, TILE)
            top[:, at] = jnp.maximum(top[:, at], jnp.max(s.reshape(2 * BLOCK // 8, 8, TILE), axis=0))
        return carry

    lax.fori_loop(0, trips, score_visit, 0)
    top[...] = jnp.broadcast_to(jnp.max(top[...], axis=0, keepdims=True), top.shape)

    def weight_visit(i, carry):
        v_t = two(i, HEAD_SIZE).T
        for w in range(WIDE // TILE):
            at = pl.ds(w * TILE, TILE)
            s = scores[pl.ds(2 * i, 2), :, at].reshape(2 * BLOCK // 8, 8, TILE)
            p = jnp.exp2(s - top[:, at][None])
            total[:, at] += jnp.sum(p, axis=0)
            low = p.reshape(2 * BLOCK, TILE).astype(BF16)
            weights[pl.ds(2 * i, 2), :, at] = low.reshape(2, BLOCK, TILE)
            turned[:, at] += dot(v_t, low)
        return carry

    lax.fori_loop(0, trips, weight_visit, 0)

    for h in range(GROUP):
        at = pl.ds(h * BLOCK, BLOCK)
        inverse = 1.0 / jnp.sum(total[:, at], axis=0, keepdims=True)
        attn = (turned[:, at] * inverse).astype(BF16)
        out_ref[0, :, at] = attn.T
        grad = (g_t[:, at].astype(F32) * inverse).astype(BF16)
        g_t[:, at] = grad
        g_s[at, :] = grad.T
        row[:, at] = jnp.broadcast_to(
            jnp.sum(grad.astype(F32) * attn.astype(F32), axis=0, keepdims=True), (8, BLOCK)
        )
    turned[...] = jnp.zeros_like(turned)

    def back_visit(i, carry):
        k = two(i, 0)
        v = two(i, HEAD_SIZE)
        k_t = k.T
        for w in range(WIDE // TILE):
            at = pl.ds(w * TILE, TILE)
            p = weights[pl.ds(2 * i, 2), :, at].reshape(2 * BLOCK, TILE).astype(F32)
            dp = dot(v, g_t[:, at])
            ds = p.reshape(2 * BLOCK // 8, 8, TILE) * (dp.reshape(2 * BLOCK // 8, 8, TILE) - row[:, at][None])
            ds = ds.reshape(2 * BLOCK, TILE).astype(BF16)
            dsc[:, at] = ds
            turned[:, at] += dot(k_t, ds)
        dk = dot(dsc[...], q_s[...])
        dv = dot(weights[pl.ds(2 * i, 2)].reshape(2 * BLOCK, WIDE), g_s[...])
        for half in range(2):
            a = pairs[t, 2 * i + half]
            rows = slice(half * BLOCK, (half + 1) * BLOCK)
            dkv[a, :, pl.ds(0, HEAD_SIZE)] += dk[rows]
            dkv[a, :, pl.ds(HEAD_SIZE, HEAD_SIZE)] += dv[rows]
        return carry

    lax.fori_loop(0, trips, back_visit, 0)

    for h in range(GROUP):
        at = pl.ds(h * BLOCK, BLOCK)
        out_ref[1, :, at] = (turned[:, at] * SCALE).astype(BF16).T

    @pl.when(t == NB - 1)
    def _():
        left, right = pl.ds(0, HEAD_SIZE), pl.ds(HEAD_SIZE, HEAD_SIZE)
        for c in range(NB):
            rows = pl.ds(c * BLOCK, BLOCK)
            own_ref[rows, left] = dkv[c, :, left] * SCALE
            own_ref[rows, right] = dkv[c, :, right]
            for s in range(1, NSTEP):
                part_refs[s - 1][rows, left] = (dkv[s * NB + c, :, left] * SCALE).astype(BF16)
                part_refs[s - 1][rows, right] = dkv[s * NB + c, :, right].astype(BF16)


def attend_call(codes, counts, place, qd, kv):
    rows = NB * BLOCK
    whole = pl.BlockSpec((rows, 2 * HEAD_SIZE), lambda t, *_: (0, 0))
    block = pl.BlockSpec((None, 2, BLOCK, WIDE), lambda t, *_: (t, 0, 0, 0))
    small = (rows, 2 * HEAD_SIZE)
    return pl.pallas_call(
        attend,
        grid_spec=pltpu.PrefetchScalarGridSpec(
            num_scalar_prefetch=3,
            grid=(NB,),
            in_specs=[block] + [whole] * NSTEP,
            out_specs=[block] + [whole] * NSTEP,
            scratch_shapes=[
                pltpu.SMEM((NB, MOST + 8), jnp.int32),
                pltpu.SMEM((NB,), jnp.int32),
                pltpu.VMEM((MOST, BLOCK, 2 * HEAD_SIZE), BF16),
                pltpu.VMEM((MOST, BLOCK, 2 * HEAD_SIZE), F32),
                pltpu.VMEM((3, BLOCK, BLOCK), F32),
                pltpu.VMEM((HEAD_SIZE, WIDE), BF16),
                pltpu.VMEM((WIDE, HEAD_SIZE), BF16),
                pltpu.VMEM((HEAD_SIZE, WIDE), BF16),
                pltpu.VMEM((WIDE, HEAD_SIZE), BF16),
                pltpu.VMEM((MOST, BLOCK, WIDE), F32),
                pltpu.VMEM((MOST, BLOCK, WIDE), BF16),
                pltpu.VMEM((8, WIDE), F32),
                pltpu.VMEM((8, WIDE), F32),
                pltpu.VMEM((8, WIDE), F32),
                pltpu.VMEM((HEAD_SIZE, WIDE), F32),
                pltpu.VMEM((2 * BLOCK, WIDE), BF16),
            ],
        ),
        out_shape=[jax.ShapeDtypeStruct(qd.shape, BF16), jax.ShapeDtypeStruct(small, F32)]
        + [jax.ShapeDtypeStruct(small, BF16)] * (NSTEP - 1),
        compiler_params=pltpu.CompilerParams(
            dimension_semantics=("arbitrary",), vmem_limit_bytes=58 * 1024 * 1024
        ),
    )(codes, counts, place, qd, *kv)


def shifted(x, distance):
    n = lax.axis_size("blk")
    return lax.ppermute(x, "blk", [((i - distance) % n, i) for i in range(n)])


def hop(x, moves):
    quads = lax.axis_size("blk") // QUAD
    return lax.ppermute(x, "blk", [(q * QUAD + a, q * QUAD + b) for q in range(quads) for a, b in moves])


UP = [(y, (y + 1) % QUAD) for y in range(QUAD)]
DOWN = [(y, (y - 1) % QUAD) for y in range(QUAD)]


def flipped(moves):
    return [(b, a) for a, b in moves]


NEAR_UP, NEAR_DOWN = [(3, 0), (0, 1)], [(3, 2), (0, 3)]
FAR_UP, FAR_DOWN = [(1, 2), (2, 3)], [(1, 0), (2, 1)]


def spread(own, y):
    prev = shifted(own, QUAD)
    back = shifted(own, 2 * QUAD)
    near_1 = hop(prev, UP)
    near_3 = hop(prev, DOWN)
    far_1 = hop(jnp.where(y == QUAD - 1, back, own), UP)
    far_3 = hop(jnp.where(y == 0, own, back), DOWN)
    near_2 = jnp.where(y < 2, hop(near_1, NEAR_UP), hop(near_3, NEAR_DOWN))
    far_2 = jnp.where(y >= 2, hop(far_1, FAR_UP), hop(far_3, FAR_DOWN))
    return (own, prev, near_1, near_3, near_2, far_1, far_3, far_2)


def plus(a, b):
    return (a.astype(F32) + b.astype(F32)).astype(BF16)


def gathered(own, parts, y):
    prev, near_1, near_3, near_2, far_1, far_3, far_2 = parts
    near_1 = plus(near_1, hop(near_2, flipped(NEAR_UP)))
    near_3 = plus(near_3, hop(near_2, flipped(NEAR_DOWN)))
    far_1 = plus(far_1, hop(far_2, flipped(FAR_UP)))
    far_3 = plus(far_3, hop(far_2, flipped(FAR_DOWN)))
    near_1 = hop(near_1, flipped(UP)).astype(F32)
    near_3 = hop(near_3, flipped(DOWN)).astype(F32)
    far_1 = hop(far_1, flipped(UP)).astype(F32)
    far_3 = hop(far_3, flipped(DOWN)).astype(F32)
    prev = (prev.astype(F32) + near_1 + near_3).astype(BF16)
    back = (jnp.where(y == QUAD - 1, far_1, 0.0) + jnp.where(y == 0, 0.0, far_3)).astype(BF16)
    own = own + jnp.where(y == QUAD - 1, 0.0, far_1) + jnp.where(y == 0, far_3, 0.0)
    return own + shifted(prev, -QUAD).astype(F32) + shifted(back, -2 * QUAD).astype(F32)


def swap(x):
    return lax.all_to_all(x, "head", split_axis=0, concat_axis=0, tiled=True)


def body(query, key, value, output_gradient, pair_codes, pair_counts):
    ranks = lax.axis_size("head")
    tokens = query.shape[0]
    held = KEY_VALUE_HEADS // ranks
    y = lax.axis_index("blk") % QUAD
    place = jnp.full((1,), y, jnp.int32)
    codes, counts = pair_codes[0], pair_counts[0]
    q_all = query.reshape(tokens, ranks, held, WIDE)
    g_all = output_gradient.reshape(tokens, ranks, held, WIDE)
    k_all = key.reshape(tokens, ranks, held, HEAD_SIZE)
    v_all = value.reshape(tokens, ranks, held, HEAD_SIZE)
    windows, rows = [], []
    for j in range(held):
        kv = jnp.concatenate([k_all[:, :, j], v_all[:, :, j]], axis=-1)
        kv = swap(jnp.transpose(kv, (1, 0, 2))).reshape(ranks * tokens, 2 * HEAD_SIZE)
        windows.append(spread(kv, y))
    for j in range(held):
        qd = jnp.stack([q_all[:, :, j], g_all[:, :, j]])
        rows.append(swap(jnp.transpose(qd, (2, 0, 1, 3))))
    outs, sums = [], []
    for j in range(held):
        both, own, *parts = attend_call(codes, counts, place, rows[j], windows[j])
        outs.append(swap(both))
        kv_sum = gathered(own, parts, y).astype(BF16)
        sums.append(swap(kv_sum.reshape(ranks, tokens, 2 * HEAD_SIZE)))
    wide = jnp.stack(outs, axis=3)
    attn_out = jnp.transpose(wide[:, 0], (1, 0, 2, 3)).reshape(query.shape)
    grad_query = jnp.transpose(wide[:, 1], (1, 0, 2, 3)).reshape(query.shape)
    small = jnp.transpose(jnp.stack(sums, axis=2), (1, 0, 2, 3))
    key_gradient = small[..., :HEAD_SIZE].reshape(key.shape)
    value_gradient = small[..., HEAD_SIZE:].reshape(value.shape)
    return attn_out, grad_query, key_gradient, value_gradient


def solution(mesh):
    rows = P(("blk", "head"), None)
    return jax.shard_map(
        body,
        mesh=mesh,
        in_specs=(rows, rows, rows, rows, P("blk", None, None), P("blk", None)),
        out_specs=(rows, rows, rows, rows),
        check_vma=False,
    )
```

```python
import jax
import jax.numpy as jnp
from jax import lax
from jax.experimental import pallas as pl
from jax.experimental.pallas import tpu as pltpu
from jax.sharding import PartitionSpec as P


QUERY_HEADS = 64
KEY_VALUE_HEADS = 8
HEAD_SIZE = 128
BLOCK = 128
NSTEP = 8
NB = 4
QUAD = 4
GROUP = QUERY_HEADS // KEY_VALUE_HEADS
WIDE = GROUP * BLOCK
MOST = NSTEP * NB
NEGATIVE_FILL = -1e30
SCALE = HEAD_SIZE ** (-0.5)
SCALE_LOG2 = SCALE * 1.4426950408889634
TILE = 256
F32 = jnp.float32
BF16 = jnp.bfloat16


def dot(a, b):
    return lax.dot_general(a, b, (((1,), (0,)), ((), ())), preferred_element_type=F32)


def dot_nt(a, b):
    return lax.dot_general(a, b, (((1,), (1,)), ((), ())), preferred_element_type=F32)


def attend(
    codes, counts, place, qd_ref, own_in, prev_in, near_1, near_2, near_3, out_ref, own_out, prev_out, part_1, part_2, part_3,
    pairs, filled, kvs, dkv, masks, q_t, g_t, scores, weights, top, total, row, turned,
):
    t = pl.program_id(0)

    @pl.when(t == 0)
    def _():
        y = place[0]
        for b in range(NB):
            pairs[b, 0] = b
            filled[b] = 1
        for s in range(NSTEP):
            d = s % QUAD
            if d == 0:
                slot = 0 if s == 0 else 1
            elif s < QUAD:
                slot = 2 * d + jnp.where(y >= d, 1, 0)
            else:
                slot = 2 * d + jnp.where(y >= d, 0, 1)

            def add(i, carry, s=s, slot=slot):
                code = codes[s, i]
                b = lax.shift_right_logical(code, 2)
                c = jnp.bitwise_and(code, 3)

                def put():
                    n = filled[b]
                    pairs[b, n] = slot * NB + c
                    filled[b] = n + 1

                if s == 0:
                    pl.when(b != c)(put)
                else:
                    put()
                return carry

            lax.fori_loop(0, counts[s], add, 0)
        for b in range(NB):
            pairs[b, filled[b]] = b
        kvs[0:NB] = own_in[...]
        kvs[NB : 2 * NB] = prev_in[...]
        for d, ref in enumerate((near_1, near_2, near_3), 1):
            for m in range(2):
                kvs[(2 * d + m) * NB : (2 * d + m + 1) * NB] = ref[m]
        dkv[...] = jnp.zeros_like(dkv)
        keys_at = lax.broadcasted_iota(jnp.int32, (BLOCK, BLOCK), 0)
        rows_at = lax.broadcasted_iota(jnp.int32, (BLOCK, BLOCK), 1)
        masks[0] = jnp.zeros((BLOCK, BLOCK), F32)
        masks[1] = jnp.where(keys_at <= rows_at, 0.0, NEGATIVE_FILL)
        masks[2] = jnp.full((BLOCK, BLOCK), NEGATIVE_FILL, F32)

    for h in range(GROUP):
        at = pl.ds(h * BLOCK, BLOCK)
        q = qd_ref[0, :, at]
        q_t[:, at] = q.T
        g_t[:, at] = qd_ref[1, :, at].T

    n = filled[t]
    trips = lax.shift_right_logical(n + 1, 1)
    top[...] = jnp.full_like(top, NEGATIVE_FILL)
    total[...] = jnp.zeros_like(total)
    turned[...] = jnp.zeros_like(turned)

    def two(i, lo):
        a, b = pairs[t, 2 * i], pairs[t, 2 * i + 1]
        return jnp.concatenate([kvs[a, :, pl.ds(lo, HEAD_SIZE)], kvs[b, :, pl.ds(lo, HEAD_SIZE)]], axis=0)

    def score_visit(i, carry):
        k = two(i, 0)
        first = masks[jnp.where(i == 0, 1, 0)]
        second = masks[jnp.where(2 * i + 1 >= n, 2, 0)]
        mask = jnp.concatenate([first, second], axis=0)
        mask = jnp.concatenate([mask, mask], axis=1)
        for w in range(WIDE // TILE):
            at = pl.ds(w * TILE, TILE)
            s = dot(k, q_t[:, at]) * SCALE_LOG2 + mask
            scores[pl.ds(2 * i, 2), :, at] = s.reshape(2, BLOCK, TILE)
            top[:, at] = jnp.maximum(top[:, at], jnp.max(s.reshape(2 * BLOCK // 8, 8, TILE), axis=0))
        return carry

    lax.fori_loop(0, trips, score_visit, 0)
    top[...] = jnp.broadcast_to(jnp.max(top[...], axis=0, keepdims=True), top.shape)

    def weight_visit(i, carry):
        v_t = two(i, HEAD_SIZE).T
        for w in range(WIDE // TILE):
            at = pl.ds(w * TILE, TILE)
            s = scores[pl.ds(2 * i, 2), :, at].reshape(2 * BLOCK // 8, 8, TILE)
            p = jnp.exp2(s - top[:, at][None])
            total[:, at] += jnp.sum(p, axis=0)
            low = p.reshape(2 * BLOCK, TILE).astype(BF16)
            weights[pl.ds(2 * i, 2), :, at] = low.reshape(2, BLOCK, TILE)
            turned[:, at] += dot(v_t, low)
        return carry

    lax.fori_loop(0, trips, weight_visit, 0)

    for h in range(GROUP):
        at = pl.ds(h * BLOCK, BLOCK)
        inverse = 1.0 / jnp.sum(total[:, at], axis=0, keepdims=True)
        attn = (turned[:, at] * inverse).astype(BF16)
        out_ref[0, :, at] = attn.T
        grad = (g_t[:, at].astype(F32) * inverse).astype(BF16)
        g_t[:, at] = grad
        row[:, at] = jnp.broadcast_to(
            jnp.sum(grad.astype(F32) * attn.astype(F32), axis=0, keepdims=True), (8, BLOCK)
        )
    turned[...] = jnp.zeros_like(turned)

    def back_visit(i, carry):
        k = two(i, 0)
        v = two(i, HEAD_SIZE)
        k_t = k.T
        tiles = [pl.ds(w * TILE, TILE) for w in range(WIDE // TILE)]
        dp = dot(v, g_t[:, tiles[0]])
        dk = dv = None
        for w, at in enumerate(tiles):
            ahead = dot(v, g_t[:, tiles[w + 1]]) if w + 1 < len(tiles) else None
            low = weights[pl.ds(2 * i, 2), :, at].reshape(2 * BLOCK, TILE)
            dv_w = dot_nt(g_t[:, at], low)
            dv = dv_w if dv is None else dv + dv_w
            p = low.astype(F32)
            ds = p.reshape(2 * BLOCK // 8, 8, TILE) * (dp.reshape(2 * BLOCK // 8, 8, TILE) - row[:, at][None])
            ds = ds.reshape(2 * BLOCK, TILE).astype(BF16)
            turned[:, at] += dot(k_t, ds)
            dk_w = dot_nt(q_t[:, at], ds)
            dk = dk_w if dk is None else dk + dk_w
            dp = ahead
        for half in range(2):
            a = pairs[t, 2 * i + half]
            columns = slice(half * BLOCK, (half + 1) * BLOCK)
            dkv[a, pl.ds(0, HEAD_SIZE)] += dk[:, columns]
            dkv[a, pl.ds(HEAD_SIZE, HEAD_SIZE)] += dv[:, columns]
        return carry

    lax.fori_loop(0, trips, back_visit, 0)

    for h in range(GROUP):
        at = pl.ds(h * BLOCK, BLOCK)
        out_ref[1, :, at] = (turned[:, at] * SCALE).astype(BF16).T

    @pl.when(t == NB - 1)
    def _():
        left, right = pl.ds(0, HEAD_SIZE), pl.ds(HEAD_SIZE, HEAD_SIZE)
        for c in range(NB):
            for at, ref in enumerate((own_out, prev_out)):
                ref[c, :, left] = (dkv[at * NB + c, left] * SCALE).T
                ref[c, :, right] = dkv[at * NB + c, right].T
            for d, ref in enumerate((part_1, part_2, part_3), 1):
                for m in range(2):
                    at = (2 * d + m) * NB + c
                    ref[m, c, :, left] = (dkv[at, left] * SCALE).astype(BF16).T
                    ref[m, c, :, right] = dkv[at, right].astype(BF16).T


def attend_call(j, codes, counts, place, qd, own, prev, near):
    mine = pl.BlockSpec((NB, None, BLOCK, 2 * HEAD_SIZE), lambda t, *_: (0, j, 0, 0))
    whole = pl.BlockSpec((2, NB, BLOCK, 2 * HEAD_SIZE), lambda t, *_: (0, 0, 0, 0))
    flat = pl.BlockSpec((NB, BLOCK, 2 * HEAD_SIZE), lambda t, *_: (0, 0, 0))
    block = pl.BlockSpec((None, 2, BLOCK, WIDE), lambda t, *_: (t, 0, 0, 0))
    return pl.pallas_call(
        attend,
        name="attend",
        grid_spec=pltpu.PrefetchScalarGridSpec(
            num_scalar_prefetch=3,
            grid=(NB,),
            in_specs=[block, mine, mine, whole, whole, whole],
            out_specs=[block, flat, flat, whole, whole, whole],
            scratch_shapes=[
                pltpu.SMEM((NB, MOST + 8), jnp.int32),
                pltpu.SMEM((NB,), jnp.int32),
                pltpu.VMEM((MOST, BLOCK, 2 * HEAD_SIZE), BF16),
                pltpu.VMEM((MOST, 2 * HEAD_SIZE, BLOCK), F32),
                pltpu.VMEM((3, BLOCK, BLOCK), F32),
                pltpu.VMEM((HEAD_SIZE, WIDE), BF16),
                pltpu.VMEM((HEAD_SIZE, WIDE), BF16),
                pltpu.VMEM((MOST, BLOCK, WIDE), F32),
                pltpu.VMEM((MOST, BLOCK, WIDE), BF16),
                pltpu.VMEM((8, WIDE), F32),
                pltpu.VMEM((8, WIDE), F32),
                pltpu.VMEM((8, WIDE), F32),
                pltpu.VMEM((HEAD_SIZE, WIDE), F32),
            ],
        ),
        out_shape=[
            jax.ShapeDtypeStruct(qd.shape, BF16),
            jax.ShapeDtypeStruct((NB, BLOCK, 2 * HEAD_SIZE), F32),
            jax.ShapeDtypeStruct((NB, BLOCK, 2 * HEAD_SIZE), F32),
        ]
        + [jax.ShapeDtypeStruct((2, NB, BLOCK, 2 * HEAD_SIZE), BF16)] * 3,
        cost_estimate=pl.CostEstimate(flops=30_000_000_000, bytes_accessed=20_000_000, transcendentals=70_000_000),
        compiler_params=pltpu.CompilerParams(
            dimension_semantics=("arbitrary",), vmem_limit_bytes=58 * 1024 * 1024
        ),
    )(codes, counts, place, qd, own, prev, *near)


def pack_rows(j, query, grad):
    def kernel(q_ref, g_ref, o_ref):
        o_ref[0] = q_ref[...]
        o_ref[1] = g_ref[...]

    tokens = query.shape[0]
    ranks = query.shape[1] // (2 * WIDE)
    column = pl.BlockSpec((tokens, WIDE), lambda r: (0, 2 * r + j))
    return pl.pallas_call(
        kernel,
        name="pack_rows",
        grid=(ranks,),
        in_specs=[column, column],
        out_specs=pl.BlockSpec((None, 2, tokens, WIDE), lambda r: (r, 0, 0, 0)),
        out_shape=jax.ShapeDtypeStruct((ranks, 2, tokens, WIDE), BF16),
    )(query, grad)


def pack_keys(key, value):
    def kernel(k_ref, v_ref, o_ref):
        for r in range(ranks):
            for j in range(2):
                at = pl.ds((2 * r + j) * HEAD_SIZE, HEAD_SIZE)
                o_ref[r, j, :, pl.ds(0, HEAD_SIZE)] = k_ref[:, at]
                o_ref[r, j, :, pl.ds(HEAD_SIZE, HEAD_SIZE)] = v_ref[:, at]

    tokens = key.shape[0]
    ranks = key.shape[1] // (2 * HEAD_SIZE)
    return pl.pallas_call(
        kernel,
        name="pack_keys",
        out_shape=jax.ShapeDtypeStruct((ranks, 2, tokens, 2 * HEAD_SIZE), BF16),
    )(key, value)


def pack_window(place, own, prev, back):
    def kernel(y_ref, own_ref, prev_ref, back_ref, *out_refs):
        for d in range(1, QUAD):
            for j in range(2):
                out = out_refs[2 * (d - 1) + j]
                out[0] = prev_ref[:, j]
                pick = y_ref[0] + d < QUAD

                @pl.when(pick)
                def _(out=out, j=j):
                    out[1] = own_ref[:, j]

                @pl.when(jnp.logical_not(pick))
                def _(out=out, j=j):
                    out[1] = back_ref[:, j]

    shape = (2,) + own.shape[:1] + own.shape[2:]
    vmem = pl.BlockSpec(memory_space=pltpu.VMEM)
    outs = pl.pallas_call(
        kernel,
        name="pack_window",
        in_specs=[pl.BlockSpec(memory_space=pltpu.SMEM), vmem, vmem, vmem],
        out_specs=[vmem] * 6,
        out_shape=[jax.ShapeDtypeStruct(shape, BF16)] * 6,
    )(place, own, prev, back)
    return [outs[j::2] for j in range(2)]


def unpack_rows(j, got, filled):
    def kernel(got_ref, *refs):
        a_ref, g_ref = refs[-2:]
        a_ref[...] = got_ref[0]
        g_ref[...] = got_ref[1]

    ranks, _, tokens, _ = got.shape
    column = pl.BlockSpec((tokens, WIDE), lambda r: (0, 2 * r + j))
    whole = jax.ShapeDtypeStruct((tokens, ranks * 2 * WIDE), BF16)
    given = () if filled is None else filled
    return pl.pallas_call(
        kernel,
        name="unpack_rows",
        grid=(ranks,),
        in_specs=[pl.BlockSpec((None, 2, tokens, WIDE), lambda r: (r, 0, 0, 0))]
        + [pl.BlockSpec(memory_space=pl.ANY)] * len(given),
        out_specs=[column, column],
        out_shape=[whole, whole],
        input_output_aliases={} if filled is None else {1: 0, 2: 1},
    )(got, *given)


def unpack_keys(got):
    def kernel(got_ref, k_ref, v_ref):
        for r in range(ranks):
            for j in range(2):
                at = pl.ds((2 * r + j) * HEAD_SIZE, HEAD_SIZE)
                k_ref[:, at] = got_ref[r, j, :, pl.ds(0, HEAD_SIZE)]
                v_ref[:, at] = got_ref[r, j, :, pl.ds(HEAD_SIZE, HEAD_SIZE)]

    ranks, _, tokens, _ = got.shape
    whole = jax.ShapeDtypeStruct((tokens, ranks * 2 * HEAD_SIZE), BF16)
    return pl.pallas_call(kernel, name="unpack_keys", out_shape=[whole, whole])(got)


def shifted(x, distance):
    n = lax.axis_size("blk")
    return lax.ppermute(x, "blk", [((i - distance) % n, i) for i in range(n)])


def turned_in_quad(x, d):
    n = lax.axis_size("blk")
    return lax.ppermute(x, "blk", [(i, i - i % QUAD + (i + d) % QUAD) for i in range(n)])


def add_parts(place, own, prev, parts):
    def kernel(y_ref, own_ref, prev_ref, *refs):
        part_refs, own_out, prev_out, back_out = refs[:-3], refs[-3], refs[-2], refs[-1]
        mine, before = own_ref[...], prev_ref[...]
        back = jnp.zeros_like(mine)
        for d, ref in enumerate(part_refs, 1):
            before = before + ref[0].astype(F32)
            other = ref[1].astype(F32)
            ahead = (y_ref[0] + d < QUAD).astype(F32)
            mine = mine + ahead * other
            back = back + (1.0 - ahead) * other
        own_out[...] = mine
        prev_out[...] = before.astype(BF16)
        back_out[...] = back.astype(BF16)

    block = (BLOCK, 2 * HEAD_SIZE)
    flat = pl.BlockSpec((None,) + block, lambda c: (c, 0, 0))
    pair = pl.BlockSpec((2, None) + block, lambda c: (0, c, 0, 0))
    return pl.pallas_call(
        kernel,
        name="add_parts",
        grid=(NB,),
        in_specs=[pl.BlockSpec(memory_space=pltpu.SMEM), flat, flat] + [pair] * len(parts),
        out_specs=[flat] * 3,
        out_shape=[
            jax.ShapeDtypeStruct(own.shape, F32),
            jax.ShapeDtypeStruct(own.shape, BF16),
            jax.ShapeDtypeStruct(own.shape, BF16),
        ],
    )(place, own, prev, *parts)


def add_home(sums):
    def kernel(*refs):
        out = refs[-1]
        for j in range(2):
            own, prev, back = (ref[...].astype(F32) for ref in refs[3 * j : 3 * j + 3])
            out[j] = (own + prev + back).astype(BF16)

    block = (BLOCK, 2 * HEAD_SIZE)
    flat = pl.BlockSpec((None,) + block, lambda c: (c, 0, 0))
    return pl.pallas_call(
        kernel,
        name="add_home",
        grid=(NB,),
        in_specs=[flat] * 6,
        out_specs=pl.BlockSpec((None, 2) + block, lambda c: (c, 0, 0, 0)),
        out_shape=jax.ShapeDtypeStruct((NB, 2) + block, BF16),
    )(*sums)


def gathered(place, own, prev, parts):
    got = [turned_in_quad(part, -d) for d, part in enumerate(parts, 1)]
    own, prev, back = add_parts(place, own, prev, got)
    return [own, shifted(prev, -QUAD), shifted(back, -2 * QUAD)]


def swap(x):
    return lax.all_to_all(x, "head", split_axis=0, concat_axis=0, tiled=True)


def layer(query, key, value, output_gradient, pair_codes, pair_counts):
    y = lax.axis_index("blk") % QUAD
    place = jnp.full((1,), y, jnp.int32)
    codes, counts = pair_codes[0], pair_counts[0]
    own = swap(pack_keys(key, value))
    prev, back = shifted(own, QUAD), shifted(own, 2 * QUAD)
    sends = pack_window(place, own, prev, back)
    near, rows = [], []
    for j in range(2):
        near.append([turned_in_quad(sends[j][d - 1], d) for d in range(1, QUAD)])
        packed = pack_rows(j, query, output_gradient)
        rows.append(swap(packed))
    filled, sums = None, []
    for j in range(2):
        both, own_sum, prev_sum, *parts = attend_call(j, codes, counts, place, rows[j], own, prev, near[j])
        got = swap(both)
        filled = unpack_rows(j, got, filled)
        sums += gathered(place, own_sum, prev_sum, parts)
    both = add_home(sums)
    got = swap(both)
    key_gradient, value_gradient = unpack_keys(got)
    return filled[0], filled[1], key_gradient, value_gradient


def solution(mesh):
    rows = P(("blk", "head"), None)
    return jax.shard_map(
        layer,
        mesh=mesh,
        in_specs=(rows, rows, rows, rows, P("blk", None, None), P("blk", None)),
        out_specs=(rows, rows, rows, rows),
        check_vma=False,
    )
```

```python
import jax
import jax.numpy as jnp
from jax import lax
from jax.experimental import pallas as pl
from jax.experimental.pallas import tpu as pltpu
from jax.sharding import PartitionSpec as P


QUERY_HEADS = 64
KEY_VALUE_HEADS = 8
HEAD_SIZE = 128
BLOCK = 128
NSTEP = 8
NB = 4
QUAD = 4
GROUP = QUERY_HEADS // KEY_VALUE_HEADS
WIDE = GROUP * BLOCK
MOST = NSTEP * NB
NEGATIVE_FILL = -1e30
SCALE = HEAD_SIZE ** (-0.5)
SCALE_LOG2 = SCALE * 1.4426950408889634
TILE = 256
F32 = jnp.float32
BF16 = jnp.bfloat16


def dot(a, b):
    return lax.dot_general(a, b, (((1,), (0,)), ((), ())), preferred_element_type=F32)


def dot_nt(a, b):
    return lax.dot_general(a, b, (((1,), (1,)), ((), ())), preferred_element_type=F32)


def attend(
    codes, counts, place, qd_ref, own_in, prev_in, near_1, near_2, near_3, out_ref, own_out, prev_out, part_1, part_2, part_3,
    pairs, filled, kvs, dkv, masks, q_t, g_t, scores, weights, top, total, row, turned,
):
    t = pl.program_id(0)

    @pl.when(t == 0)
    def _():
        y = place[0]
        for b in range(NB):
            pairs[b, 0] = b
            filled[b] = 1
        for s in range(NSTEP):
            d = s % QUAD
            if d == 0:
                slot = 0 if s == 0 else 1
            elif s < QUAD:
                slot = 2 * d + jnp.where(y >= d, 1, 0)
            else:
                slot = 2 * d + jnp.where(y >= d, 0, 1)

            def add(i, carry, s=s, slot=slot):
                code = codes[s, i]
                b = lax.shift_right_logical(code, 2)
                c = jnp.bitwise_and(code, 3)

                def put():
                    n = filled[b]
                    pairs[b, n] = slot * NB + c
                    filled[b] = n + 1

                if s == 0:
                    pl.when(b != c)(put)
                else:
                    put()
                return carry

            lax.fori_loop(0, counts[s], add, 0)
        for b in range(NB):
            pairs[b, filled[b]] = b
        kvs[0:NB] = own_in[...]
        kvs[NB : 2 * NB] = prev_in[...]
        for d, ref in enumerate((near_1, near_2, near_3), 1):
            for m in range(2):
                kvs[(2 * d + m) * NB : (2 * d + m + 1) * NB] = ref[m]
        dkv[...] = jnp.zeros_like(dkv)
        keys_at = lax.broadcasted_iota(jnp.int32, (BLOCK, BLOCK), 0)
        rows_at = lax.broadcasted_iota(jnp.int32, (BLOCK, BLOCK), 1)
        masks[0] = jnp.zeros((BLOCK, BLOCK), F32)
        masks[1] = jnp.where(keys_at <= rows_at, 0.0, NEGATIVE_FILL)
        masks[2] = jnp.full((BLOCK, BLOCK), NEGATIVE_FILL, F32)

    for h in range(GROUP):
        at = pl.ds(h * BLOCK, BLOCK)
        q = qd_ref[0, :, at]
        q_t[:, at] = q.T
        g_t[:, at] = qd_ref[1, :, at].T

    n = filled[t]
    trips = lax.shift_right_logical(n + 1, 1)
    top[...] = jnp.full_like(top, NEGATIVE_FILL)
    total[...] = jnp.zeros_like(total)
    turned[...] = jnp.zeros_like(turned)

    def two(i, lo):
        a, b = pairs[t, 2 * i], pairs[t, 2 * i + 1]
        return jnp.concatenate([kvs[a, :, pl.ds(lo, HEAD_SIZE)], kvs[b, :, pl.ds(lo, HEAD_SIZE)]], axis=0)

    def score_visit(i, carry):
        k = two(i, 0)
        first = masks[jnp.where(i == 0, 1, 0)]
        second = masks[jnp.where(2 * i + 1 >= n, 2, 0)]
        mask = jnp.concatenate([first, second], axis=0)
        mask = jnp.concatenate([mask, mask], axis=1)
        for w in range(WIDE // TILE):
            at = pl.ds(w * TILE, TILE)
            s = dot(k, q_t[:, at]) * SCALE_LOG2 + mask
            scores[pl.ds(2 * i, 2), :, at] = s.reshape(2, BLOCK, TILE)
            top[:, at] = jnp.maximum(top[:, at], jnp.max(s.reshape(2 * BLOCK // 8, 8, TILE), axis=0))
        return carry

    lax.fori_loop(0, trips, score_visit, 0)
    top[...] = jnp.broadcast_to(jnp.max(top[...], axis=0, keepdims=True), top.shape)

    def weight_visit(i, carry):
        v_t = two(i, HEAD_SIZE).T
        for w in range(WIDE // TILE):
            at = pl.ds(w * TILE, TILE)
            s = scores[pl.ds(2 * i, 2), :, at].reshape(2 * BLOCK // 8, 8, TILE)
            p = jnp.exp2(s - top[:, at][None])
            total[:, at] += jnp.sum(p, axis=0)
            low = p.reshape(2 * BLOCK, TILE).astype(BF16)
            weights[pl.ds(2 * i, 2), :, at] = low.reshape(2, BLOCK, TILE)
            turned[:, at] += dot(v_t, low)
        return carry

    lax.fori_loop(0, trips, weight_visit, 0)

    for h in range(GROUP):
        at = pl.ds(h * BLOCK, BLOCK)
        inverse = 1.0 / jnp.sum(total[:, at], axis=0, keepdims=True)
        attn = (turned[:, at] * inverse).astype(BF16)
        out_ref[0, :, at] = attn.T
        grad = (g_t[:, at].astype(F32) * inverse).astype(BF16)
        g_t[:, at] = grad
        row[:, at] = jnp.broadcast_to(
            jnp.sum(grad.astype(F32) * attn.astype(F32), axis=0, keepdims=True), (8, BLOCK)
        )
    turned[...] = jnp.zeros_like(turned)

    def back_visit(i, carry):
        k = two(i, 0)
        v = two(i, HEAD_SIZE)
        k_t = k.T
        tiles = [pl.ds(w * TILE, TILE) for w in range(WIDE // TILE)]
        dp = dot(v, g_t[:, tiles[0]])
        dk = dv = None
        for w, at in enumerate(tiles):
            ahead = dot(v, g_t[:, tiles[w + 1]]) if w + 1 < len(tiles) else None
            low = weights[pl.ds(2 * i, 2), :, at].reshape(2 * BLOCK, TILE)
            dv_w = dot_nt(g_t[:, at], low)
            dv = dv_w if dv is None else dv + dv_w
            p = low.astype(F32)
            ds = p.reshape(2 * BLOCK // 8, 8, TILE) * (dp.reshape(2 * BLOCK // 8, 8, TILE) - row[:, at][None])
            ds = ds.reshape(2 * BLOCK, TILE).astype(BF16)
            turned[:, at] += dot(k_t, ds)
            dk_w = dot_nt(q_t[:, at], ds)
            dk = dk_w if dk is None else dk + dk_w
            dp = ahead
        for half in range(2):
            a = pairs[t, 2 * i + half]
            columns = slice(half * BLOCK, (half + 1) * BLOCK)
            dkv[a, pl.ds(0, HEAD_SIZE)] += dk[:, columns]
            dkv[a, pl.ds(HEAD_SIZE, HEAD_SIZE)] += dv[:, columns]
        return carry

    lax.fori_loop(0, trips, back_visit, 0)

    for h in range(GROUP):
        at = pl.ds(h * BLOCK, BLOCK)
        out_ref[1, :, at] = (turned[:, at] * SCALE).astype(BF16).T

    @pl.when(t == NB - 1)
    def _():
        left, right = pl.ds(0, HEAD_SIZE), pl.ds(HEAD_SIZE, HEAD_SIZE)
        for c in range(NB):
            for at, ref in enumerate((own_out, prev_out)):
                ref[c, :, left] = (dkv[at * NB + c, left] * SCALE).T
                ref[c, :, right] = dkv[at * NB + c, right].T
            for d, ref in enumerate((part_1, part_2, part_3), 1):
                for m in range(2):
                    at = (2 * d + m) * NB + c
                    ref[m, c, :, left] = (dkv[at, left] * SCALE).astype(BF16).T
                    ref[m, c, :, right] = dkv[at, right].astype(BF16).T


def attend_call(codes, counts, place, qd, own, prev, near):
    whole = pl.BlockSpec((2, NB, BLOCK, 2 * HEAD_SIZE), lambda t, *_: (0, 0, 0, 0))
    flat = pl.BlockSpec((NB, BLOCK, 2 * HEAD_SIZE), lambda t, *_: (0, 0, 0))
    block = pl.BlockSpec((None, 2, BLOCK, WIDE), lambda t, *_: (t, 0, 0, 0))
    return pl.pallas_call(
        attend,
        name="attend",
        grid_spec=pltpu.PrefetchScalarGridSpec(
            num_scalar_prefetch=3,
            grid=(NB,),
            in_specs=[block, flat, flat, whole, whole, whole],
            out_specs=[block, flat, flat, whole, whole, whole],
            scratch_shapes=[
                pltpu.SMEM((NB, MOST + 8), jnp.int32),
                pltpu.SMEM((NB,), jnp.int32),
                pltpu.VMEM((MOST, BLOCK, 2 * HEAD_SIZE), BF16),
                pltpu.VMEM((MOST, 2 * HEAD_SIZE, BLOCK), F32),
                pltpu.VMEM((3, BLOCK, BLOCK), F32),
                pltpu.VMEM((HEAD_SIZE, WIDE), BF16),
                pltpu.VMEM((HEAD_SIZE, WIDE), BF16),
                pltpu.VMEM((MOST, BLOCK, WIDE), F32),
                pltpu.VMEM((MOST, BLOCK, WIDE), BF16),
                pltpu.VMEM((8, WIDE), F32),
                pltpu.VMEM((8, WIDE), F32),
                pltpu.VMEM((8, WIDE), F32),
                pltpu.VMEM((HEAD_SIZE, WIDE), F32),
            ],
        ),
        out_shape=[
            jax.ShapeDtypeStruct(qd.shape, BF16),
            jax.ShapeDtypeStruct((NB, BLOCK, 2 * HEAD_SIZE), F32),
            jax.ShapeDtypeStruct((NB, BLOCK, 2 * HEAD_SIZE), F32),
        ]
        + [jax.ShapeDtypeStruct((2, NB, BLOCK, 2 * HEAD_SIZE), BF16)] * 3,
        cost_estimate=pl.CostEstimate(flops=30_000_000_000, bytes_accessed=20_000_000, transcendentals=70_000_000),
        compiler_params=pltpu.CompilerParams(dimension_semantics=("arbitrary",), vmem_limit_bytes=58 * 1024 * 1024),
    )(codes, counts, place, qd, own, prev, *near)


def pack_rows(j, query, grad):
    def kernel(q_ref, g_ref, o_ref):
        o_ref[0] = q_ref[...]
        o_ref[1] = g_ref[...]

    tokens = query.shape[0]
    ranks = query.shape[1] // (2 * WIDE)
    column = pl.BlockSpec((tokens, WIDE), lambda r: (0, 2 * r + j))
    return pl.pallas_call(
        kernel,
        name="pack_rows",
        grid=(ranks,),
        in_specs=[column, column],
        out_specs=pl.BlockSpec((None, 2, tokens, WIDE), lambda r: (r, 0, 0, 0)),
        out_shape=jax.ShapeDtypeStruct((ranks, 2, tokens, WIDE), BF16),
    )(query, grad)


def pack_keys(key, value):
    def kernel(k_ref, v_ref, o_ref):
        for r in range(ranks):
            for j in range(2):
                at = pl.ds((2 * r + j) * HEAD_SIZE, HEAD_SIZE)
                o_ref[r, j, :, pl.ds(0, HEAD_SIZE)] = k_ref[:, at]
                o_ref[r, j, :, pl.ds(HEAD_SIZE, HEAD_SIZE)] = v_ref[:, at]

    tokens = key.shape[0]
    ranks = key.shape[1] // (2 * HEAD_SIZE)
    return pl.pallas_call(
        kernel,
        name="pack_keys",
        out_shape=jax.ShapeDtypeStruct((ranks, 2, tokens, 2 * HEAD_SIZE), BF16),
    )(key, value)


def pack_window(place, own, prev, back):
    def kernel(y_ref, own_ref, prev_ref, back_ref, *out_refs):
        for d, out in enumerate(out_refs, 1):
            out[0] = prev_ref[...]
            pick = y_ref[0] + d < QUAD

            @pl.when(pick)
            def _(out=out):
                out[1] = own_ref[...]

            @pl.when(jnp.logical_not(pick))
            def _(out=out):
                out[1] = back_ref[...]

    vmem = pl.BlockSpec(memory_space=pltpu.VMEM)
    return pl.pallas_call(
        kernel,
        name="pack_window",
        in_specs=[pl.BlockSpec(memory_space=pltpu.SMEM), vmem, vmem, vmem],
        out_specs=[vmem] * 3,
        out_shape=[jax.ShapeDtypeStruct((2,) + own.shape, BF16)] * 3,
    )(place, own, prev, back)


def unpack_rows(j, got, filled):
    def kernel(got_ref, *refs):
        a_ref, g_ref = refs[-2:]
        a_ref[...] = got_ref[0]
        g_ref[...] = got_ref[1]

    ranks, _, tokens, _ = got.shape
    column = pl.BlockSpec((tokens, WIDE), lambda r: (0, 2 * r + j))
    whole = jax.ShapeDtypeStruct((tokens, ranks * 2 * WIDE), BF16)
    given = () if filled is None else filled
    return pl.pallas_call(
        kernel,
        name="unpack_rows",
        grid=(ranks,),
        in_specs=[pl.BlockSpec((None, 2, tokens, WIDE), lambda r: (r, 0, 0, 0))]
        + [pl.BlockSpec(memory_space=pl.ANY)] * len(given),
        out_specs=[column, column],
        out_shape=[whole, whole],
        input_output_aliases={} if filled is None else {1: 0, 2: 1},
    )(got, *given)


def unpack_keys(got):
    def kernel(got_ref, k_ref, v_ref):
        for r in range(ranks):
            for j in range(2):
                at = pl.ds((2 * r + j) * HEAD_SIZE, HEAD_SIZE)
                k_ref[:, at] = got_ref[r, j, :, pl.ds(0, HEAD_SIZE)]
                v_ref[:, at] = got_ref[r, j, :, pl.ds(HEAD_SIZE, HEAD_SIZE)]

    ranks, _, tokens, _ = got.shape
    whole = jax.ShapeDtypeStruct((tokens, ranks * 2 * HEAD_SIZE), BF16)
    return pl.pallas_call(kernel, name="unpack_keys", out_shape=[whole, whole])(got)


def shifted(x, distance):
    n = lax.axis_size("blk")
    return lax.ppermute(x, "blk", [((i - distance) % n, i) for i in range(n)])


def turned_in_quad(x, d):
    n = lax.axis_size("blk")
    return lax.ppermute(x, "blk", [(i, i - i % QUAD + (i + d) % QUAD) for i in range(n)])


def add_parts(place, own, prev, parts):
    def kernel(y_ref, own_ref, prev_ref, *refs):
        part_refs, own_out, prev_out, back_out = refs[:-3], refs[-3], refs[-2], refs[-1]
        mine, before = own_ref[...], prev_ref[...]
        back = jnp.zeros_like(mine)
        for d, ref in enumerate(part_refs, 1):
            before = before + ref[0].astype(F32)
            other = ref[1].astype(F32)
            ahead = (y_ref[0] + d < QUAD).astype(F32)
            mine = mine + ahead * other
            back = back + (1.0 - ahead) * other
        own_out[...] = mine
        prev_out[...] = before.astype(BF16)
        back_out[...] = back.astype(BF16)

    block = (BLOCK, 2 * HEAD_SIZE)
    flat = pl.BlockSpec((None,) + block, lambda c: (c, 0, 0))
    pair = pl.BlockSpec((2, None) + block, lambda c: (0, c, 0, 0))
    return pl.pallas_call(
        kernel,
        name="add_parts",
        grid=(NB,),
        in_specs=[pl.BlockSpec(memory_space=pltpu.SMEM), flat, flat] + [pair] * len(parts),
        out_specs=[flat] * 3,
        out_shape=[
            jax.ShapeDtypeStruct(own.shape, F32),
            jax.ShapeDtypeStruct(own.shape, BF16),
            jax.ShapeDtypeStruct(own.shape, BF16),
        ],
    )(place, own, prev, *parts)


def add_home(sums):
    def kernel(*refs):
        out = refs[-1]
        for j in range(2):
            own, prev, back = (ref[...].astype(F32) for ref in refs[3 * j : 3 * j + 3])
            out[j] = (own + prev + back).astype(BF16)

    block = (BLOCK, 2 * HEAD_SIZE)
    flat = pl.BlockSpec((None,) + block, lambda c: (c, 0, 0))
    return pl.pallas_call(
        kernel,
        name="add_home",
        grid=(NB,),
        in_specs=[flat] * 6,
        out_specs=pl.BlockSpec((None, 2) + block, lambda c: (c, 0, 0, 0)),
        out_shape=jax.ShapeDtypeStruct((NB, 2) + block, BF16),
    )(*sums)


def gathered(place, own, prev, parts):
    got = [turned_in_quad(part, -d) for d, part in enumerate(parts, 1)]
    own, prev, back = add_parts(place, own, prev, got)
    return [own, shifted(prev, -QUAD), shifted(back, -2 * QUAD)]


def swap(x):
    return lax.all_to_all(x, "head", split_axis=0, concat_axis=0, tiled=True)


def layer(query, key, value, output_gradient, pair_codes, pair_counts):
    y = lax.axis_index("blk") % QUAD
    place = jnp.full((1,), y, jnp.int32)
    codes, counts = pair_codes[0], pair_counts[0]
    keys = swap(pack_keys(key, value))
    packed = []
    for j in range(2):
        packed.append(pack_rows(j, query, output_gradient))
    own, prev, near, rows = [], [], [], []
    for j in range(2):
        own.append(keys[:, j])
        prev.append(shifted(own[j], QUAD))
        back = shifted(own[j], 2 * QUAD)
        sends = pack_window(place, own[j], prev[j], back)
        near.append([turned_in_quad(sends[d - 1], d) for d in range(1, QUAD)])
        rows.append(swap(packed[j]))
    filled, sums = None, []
    for j in range(2):
        both, own_sum, prev_sum, *parts = attend_call(codes, counts, place, rows[j], own[j], prev[j], near[j])
        got = swap(both)
        filled = unpack_rows(j, got, filled)
        sums += gathered(place, own_sum, prev_sum, parts)
    both = add_home(sums)
    got = swap(both)
    key_gradient, value_gradient = unpack_keys(got)
    return filled[0], filled[1], key_gradient, value_gradient


def solution(mesh):
    rows = P(("blk", "head"), None)
    return jax.shard_map(
        layer,
        mesh=mesh,
        in_specs=(rows, rows, rows, rows, P("blk", None, None), P("blk", None)),
        out_specs=(rows, rows, rows, rows),
        check_vma=False,
    )
```

```python
import jax
import jax.numpy as jnp
from jax import lax
from jax.experimental import pallas as pl
from jax.experimental.pallas import tpu as pltpu
from jax.sharding import PartitionSpec as P


QUERY_HEADS = 64
KEY_VALUE_HEADS = 8
HEAD_SIZE = 128
BLOCK = 128
NSTEP = 8
NB = 4
QUAD = 4
GROUP = QUERY_HEADS // KEY_VALUE_HEADS
WIDE = GROUP * BLOCK
MOST = NSTEP * NB
NEGATIVE_FILL = -1e30
SCALE = HEAD_SIZE ** (-0.5)
SCALE_LOG2 = SCALE * 1.4426950408889634
TILE = 256
F32 = jnp.float32
BF16 = jnp.bfloat16


def dot(a, b):
    return lax.dot_general(a, b, (((1,), (0,)), ((), ())), preferred_element_type=F32)


def dot_nt(a, b):
    return lax.dot_general(a, b, (((1,), (1,)), ((), ())), preferred_element_type=F32)


def attend(
    codes, counts, place, qd_ref, own_in, prev_in, near_1, near_2, near_3, out_ref, own_out, prev_out, part_1, part_2, part_3,
    pairs, filled, kvs, dkv, masks, q_t, g_t, scores, weights, top, total, row, turned,
):
    t = pl.program_id(0)

    @pl.when(t == 0)
    def _():
        y = place[0]
        for b in range(NB):
            pairs[b, 0] = b
            filled[b] = 1
        for s in range(NSTEP):
            d = s % QUAD
            if d == 0:
                slot = 0 if s == 0 else 1
            elif s < QUAD:
                slot = 2 * d + jnp.where(y >= d, 1, 0)
            else:
                slot = 2 * d + jnp.where(y >= d, 0, 1)

            def add(i, carry, s=s, slot=slot):
                code = codes[s, i]
                b = lax.shift_right_logical(code, 2)
                c = jnp.bitwise_and(code, 3)

                def put():
                    n = filled[b]
                    pairs[b, n] = slot * NB + c
                    filled[b] = n + 1

                if s == 0:
                    pl.when(b != c)(put)
                else:
                    put()
                return carry

            lax.fori_loop(0, counts[s], add, 0)
        for b in range(NB):
            pairs[b, filled[b]] = b
        kvs[0:NB] = own_in[...]
        kvs[NB : 2 * NB] = prev_in[...]
        for d, ref in enumerate((near_1, near_2, near_3), 1):
            for m in range(2):
                kvs[(2 * d + m) * NB : (2 * d + m + 1) * NB] = ref[m]
        dkv[...] = jnp.zeros_like(dkv)
        keys_at = lax.broadcasted_iota(jnp.int32, (BLOCK, BLOCK), 0)
        rows_at = lax.broadcasted_iota(jnp.int32, (BLOCK, BLOCK), 1)
        masks[0] = jnp.zeros((BLOCK, BLOCK), F32)
        masks[1] = jnp.where(keys_at <= rows_at, 0.0, NEGATIVE_FILL)
        masks[2] = jnp.full((BLOCK, BLOCK), NEGATIVE_FILL, F32)

    for h in range(GROUP):
        at = pl.ds(h * BLOCK, BLOCK)
        q = qd_ref[0, :, at]
        q_t[:, at] = q.T
        g_t[:, at] = qd_ref[1, :, at].T

    n = filled[t]
    trips = lax.shift_right_logical(n + 1, 1)
    top[...] = jnp.full_like(top, NEGATIVE_FILL)
    total[...] = jnp.zeros_like(total)
    turned[...] = jnp.zeros_like(turned)

    def two(i, lo):
        a, b = pairs[t, 2 * i], pairs[t, 2 * i + 1]
        return jnp.concatenate([kvs[a, :, pl.ds(lo, HEAD_SIZE)], kvs[b, :, pl.ds(lo, HEAD_SIZE)]], axis=0)

    def score_visit(i, carry):
        k = two(i, 0)
        first = masks[jnp.where(i == 0, 1, 0)]
        second = masks[jnp.where(2 * i + 1 >= n, 2, 0)]
        mask = jnp.concatenate([first, second], axis=0)
        mask = jnp.concatenate([mask, mask], axis=1)
        for w in range(WIDE // TILE):
            at = pl.ds(w * TILE, TILE)
            s = dot(k, q_t[:, at]) * SCALE_LOG2 + mask
            scores[pl.ds(2 * i, 2), :, at] = s.reshape(2, BLOCK, TILE)
            top[:, at] = jnp.maximum(top[:, at], jnp.max(s.reshape(2 * BLOCK // 8, 8, TILE), axis=0))
        return carry

    lax.fori_loop(0, trips, score_visit, 0)
    top[...] = jnp.broadcast_to(jnp.max(top[...], axis=0, keepdims=True), top.shape)

    def weight_visit(i, carry):
        v_t = two(i, HEAD_SIZE).T
        for w in range(WIDE // TILE):
            at = pl.ds(w * TILE, TILE)
            s = scores[pl.ds(2 * i, 2), :, at].reshape(2 * BLOCK // 8, 8, TILE)
            p = jnp.exp2(s - top[:, at][None])
            total[:, at] += jnp.sum(p, axis=0)
            low = p.reshape(2 * BLOCK, TILE).astype(BF16)
            weights[pl.ds(2 * i, 2), :, at] = low.reshape(2, BLOCK, TILE)
            turned[:, at] += dot(v_t, low)
        return carry

    lax.fori_loop(0, trips, weight_visit, 0)

    for h in range(GROUP):
        at = pl.ds(h * BLOCK, BLOCK)
        inverse = 1.0 / jnp.sum(total[:, at], axis=0, keepdims=True)
        attn = (turned[:, at] * inverse).astype(BF16)
        out_ref[0, :, at] = attn.T
        grad = (g_t[:, at].astype(F32) * inverse).astype(BF16)
        g_t[:, at] = grad
        row[:, at] = jnp.broadcast_to(
            jnp.sum(grad.astype(F32) * attn.astype(F32), axis=0, keepdims=True), (8, BLOCK)
        )
    turned[...] = jnp.zeros_like(turned)

    def back_visit(i, carry):
        k = two(i, 0)
        v = two(i, HEAD_SIZE)
        k_t = k.T
        tiles = [pl.ds(w * TILE, TILE) for w in range(WIDE // TILE)]
        dp = dot(v, g_t[:, tiles[0]])
        dk = dv = None
        for w, at in enumerate(tiles):
            ahead = dot(v, g_t[:, tiles[w + 1]]) if w + 1 < len(tiles) else None
            low = weights[pl.ds(2 * i, 2), :, at].reshape(2 * BLOCK, TILE)
            dv_w = dot_nt(g_t[:, at], low)
            dv = dv_w if dv is None else dv + dv_w
            p = low.astype(F32)
            ds = p.reshape(2 * BLOCK // 8, 8, TILE) * (dp.reshape(2 * BLOCK // 8, 8, TILE) - row[:, at][None])
            ds = ds.reshape(2 * BLOCK, TILE).astype(BF16)
            turned[:, at] += dot(k_t, ds)
            dk_w = dot_nt(q_t[:, at], ds)
            dk = dk_w if dk is None else dk + dk_w
            dp = ahead
        for half in range(2):
            a = pairs[t, 2 * i + half]
            columns = slice(half * BLOCK, (half + 1) * BLOCK)
            dkv[a, pl.ds(0, HEAD_SIZE)] += dk[:, columns]
            dkv[a, pl.ds(HEAD_SIZE, HEAD_SIZE)] += dv[:, columns]
        return carry

    lax.fori_loop(0, trips, back_visit, 0)

    for h in range(GROUP):
        at = pl.ds(h * BLOCK, BLOCK)
        out_ref[1, :, at] = (turned[:, at] * SCALE).astype(BF16).T

    @pl.when(t == NB - 1)
    def _():
        upper, lower = pl.ds(0, HEAD_SIZE), pl.ds(HEAD_SIZE, HEAD_SIZE)
        for c in range(NB):
            for at, ref in enumerate((own_out, prev_out)):
                ref[c, upper] = dkv[at * NB + c, upper] * SCALE
                ref[c, lower] = dkv[at * NB + c, lower]
            for d, ref in enumerate((part_1, part_2, part_3), 1):
                for m in range(2):
                    at = (2 * d + m) * NB + c
                    ref[m, c, upper] = (dkv[at, upper] * SCALE).astype(BF16)
                    ref[m, c, lower] = dkv[at, lower].astype(BF16)


def attend_call(codes, counts, place, qd, own, prev, near):
    whole = pl.BlockSpec((2, NB, BLOCK, 2 * HEAD_SIZE), lambda t, *_: (0, 0, 0, 0))
    flat = pl.BlockSpec((NB, BLOCK, 2 * HEAD_SIZE), lambda t, *_: (0, 0, 0))
    whole_t = pl.BlockSpec((2, NB, 2 * HEAD_SIZE, BLOCK), lambda t, *_: (0, 0, 0, 0))
    flat_t = pl.BlockSpec((NB, 2 * HEAD_SIZE, BLOCK), lambda t, *_: (0, 0, 0))
    block = pl.BlockSpec((None, 2, BLOCK, WIDE), lambda t, *_: (t, 0, 0, 0))
    return pl.pallas_call(
        attend,
        name="attend",
        grid_spec=pltpu.PrefetchScalarGridSpec(
            num_scalar_prefetch=3,
            grid=(NB,),
            in_specs=[block, flat, flat, whole, whole, whole],
            out_specs=[block, flat_t, flat_t, whole_t, whole_t, whole_t],
            scratch_shapes=[
                pltpu.SMEM((NB, MOST + 8), jnp.int32),
                pltpu.SMEM((NB,), jnp.int32),
                pltpu.VMEM((MOST, BLOCK, 2 * HEAD_SIZE), BF16),
                pltpu.VMEM((MOST, 2 * HEAD_SIZE, BLOCK), F32),
                pltpu.VMEM((3, BLOCK, BLOCK), F32),
                pltpu.VMEM((HEAD_SIZE, WIDE), BF16),
                pltpu.VMEM((HEAD_SIZE, WIDE), BF16),
                pltpu.VMEM((MOST, BLOCK, WIDE), F32),
                pltpu.VMEM((MOST, BLOCK, WIDE), BF16),
                pltpu.VMEM((8, WIDE), F32),
                pltpu.VMEM((8, WIDE), F32),
                pltpu.VMEM((8, WIDE), F32),
                pltpu.VMEM((HEAD_SIZE, WIDE), F32),
            ],
        ),
        out_shape=[
            jax.ShapeDtypeStruct(qd.shape, BF16),
            jax.ShapeDtypeStruct((NB, 2 * HEAD_SIZE, BLOCK), F32),
            jax.ShapeDtypeStruct((NB, 2 * HEAD_SIZE, BLOCK), F32),
        ]
        + [jax.ShapeDtypeStruct((2, NB, 2 * HEAD_SIZE, BLOCK), BF16)] * 3,
        cost_estimate=pl.CostEstimate(flops=30_000_000_000, bytes_accessed=20_000_000, transcendentals=70_000_000),
        compiler_params=pltpu.CompilerParams(dimension_semantics=("arbitrary",), vmem_limit_bytes=58 * 1024 * 1024),
    )(codes, counts, place, qd, own, prev, *near)


def pack_rows(j, query, grad):
    def kernel(q_ref, g_ref, o_ref):
        o_ref[0] = q_ref[...]
        o_ref[1] = g_ref[...]

    tokens = query.shape[0]
    ranks = query.shape[1] // (2 * WIDE)
    column = pl.BlockSpec((tokens, WIDE), lambda r: (0, 2 * r + j))
    return pl.pallas_call(
        kernel,
        name="pack_rows",
        grid=(ranks,),
        in_specs=[column, column],
        out_specs=pl.BlockSpec((None, 2, tokens, WIDE), lambda r: (r, 0, 0, 0)),
        out_shape=jax.ShapeDtypeStruct((ranks, 2, tokens, WIDE), BF16),
    )(query, grad)


def pack_keys(key, value):
    def kernel(k_ref, v_ref, o_ref):
        for r in range(ranks):
            for j in range(2):
                at = pl.ds((2 * r + j) * HEAD_SIZE, HEAD_SIZE)
                o_ref[r, j, :, pl.ds(0, HEAD_SIZE)] = k_ref[:, at]
                o_ref[r, j, :, pl.ds(HEAD_SIZE, HEAD_SIZE)] = v_ref[:, at]

    tokens = key.shape[0]
    ranks = key.shape[1] // (2 * HEAD_SIZE)
    return pl.pallas_call(
        kernel,
        name="pack_keys",
        out_shape=jax.ShapeDtypeStruct((ranks, 2, tokens, 2 * HEAD_SIZE), BF16),
    )(key, value)


def pack_window(place, own, prev, back):
    def kernel(y_ref, own_ref, prev_ref, back_ref, *out_refs):
        for d, out in enumerate(out_refs, 1):
            out[0] = prev_ref[...]
            pick = y_ref[0] + d < QUAD

            @pl.when(pick)
            def _(out=out):
                out[1] = own_ref[...]

            @pl.when(jnp.logical_not(pick))
            def _(out=out):
                out[1] = back_ref[...]

    vmem = pl.BlockSpec(memory_space=pltpu.VMEM)
    return pl.pallas_call(
        kernel,
        name="pack_window",
        in_specs=[pl.BlockSpec(memory_space=pltpu.SMEM), vmem, vmem, vmem],
        out_specs=[vmem] * 3,
        out_shape=[jax.ShapeDtypeStruct((2,) + own.shape, BF16)] * 3,
    )(place, own, prev, back)


def unpack_rows(j, got, filled):
    def kernel(got_ref, *refs):
        a_ref, g_ref = refs[-2:]
        a_ref[...] = got_ref[0]
        g_ref[...] = got_ref[1]

    ranks, _, tokens, _ = got.shape
    column = pl.BlockSpec((tokens, WIDE), lambda r: (0, 2 * r + j))
    whole = jax.ShapeDtypeStruct((tokens, ranks * 2 * WIDE), BF16)
    given = () if filled is None else filled
    return pl.pallas_call(
        kernel,
        name="unpack_rows",
        grid=(ranks,),
        in_specs=[pl.BlockSpec((None, 2, tokens, WIDE), lambda r: (r, 0, 0, 0))]
        + [pl.BlockSpec(memory_space=pl.ANY)] * len(given),
        out_specs=[column, column],
        out_shape=[whole, whole],
        input_output_aliases={} if filled is None else {1: 0, 2: 1},
    )(got, *given)


def unpack_keys(got):
    def kernel(got_ref, k_ref, v_ref):
        for r in range(ranks):
            for j in range(2):
                at = pl.ds((2 * r + j) * HEAD_SIZE, HEAD_SIZE)
                k_ref[:, at] = got_ref[r, j, :, pl.ds(0, HEAD_SIZE)]
                v_ref[:, at] = got_ref[r, j, :, pl.ds(HEAD_SIZE, HEAD_SIZE)]

    ranks, _, tokens, _ = got.shape
    whole = jax.ShapeDtypeStruct((tokens, ranks * 2 * HEAD_SIZE), BF16)
    return pl.pallas_call(kernel, name="unpack_keys", out_shape=[whole, whole])(got)


def shifted(x, distance):
    n = lax.axis_size("blk")
    return lax.ppermute(x, "blk", [((i - distance) % n, i) for i in range(n)])


def turned_in_quad(x, d):
    n = lax.axis_size("blk")
    return lax.ppermute(x, "blk", [(i, i - i % QUAD + (i + d) % QUAD) for i in range(n)])


def add_parts(place, own, prev, parts):
    def kernel(y_ref, own_ref, prev_ref, *refs):
        part_refs, own_out, prev_out, back_out = refs[:-3], refs[-3], refs[-2], refs[-1]
        mine, before = own_ref[...], prev_ref[...]
        back = jnp.zeros_like(mine)
        for d, ref in enumerate(part_refs, 1):
            before = before + ref[0].astype(F32)
            other = ref[1].astype(F32)
            ahead = (y_ref[0] + d < QUAD).astype(F32)
            mine = mine + ahead * other
            back = back + (1.0 - ahead) * other
        own_out[...] = mine
        prev_out[...] = before.astype(BF16)
        back_out[...] = back.astype(BF16)

    block = (2 * HEAD_SIZE, BLOCK)
    flat = pl.BlockSpec((None,) + block, lambda c: (c, 0, 0))
    pair = pl.BlockSpec((2, None) + block, lambda c: (0, c, 0, 0))
    return pl.pallas_call(
        kernel,
        name="add_parts",
        grid=(NB,),
        in_specs=[pl.BlockSpec(memory_space=pltpu.SMEM), flat, flat] + [pair] * len(parts),
        out_specs=[flat] * 3,
        out_shape=[
            jax.ShapeDtypeStruct(own.shape, F32),
            jax.ShapeDtypeStruct(own.shape, BF16),
            jax.ShapeDtypeStruct(own.shape, BF16),
        ],
    )(place, own, prev, *parts)


def add_home(sums):
    def kernel(*refs):
        out = refs[-1]
        for j in range(2):
            own, prev, back = (ref[...].astype(F32) for ref in refs[3 * j : 3 * j + 3])
            low = (own + prev + back).astype(BF16)
            out[j, :, pl.ds(0, HEAD_SIZE)] = low[:HEAD_SIZE].T
            out[j, :, pl.ds(HEAD_SIZE, HEAD_SIZE)] = low[HEAD_SIZE:].T

    block = (BLOCK, 2 * HEAD_SIZE)
    flat = pl.BlockSpec((None, 2 * HEAD_SIZE, BLOCK), lambda c: (c, 0, 0))
    return pl.pallas_call(
        kernel,
        name="add_home",
        grid=(NB,),
        in_specs=[flat] * 6,
        out_specs=pl.BlockSpec((None, 2) + block, lambda c: (c, 0, 0, 0)),
        out_shape=jax.ShapeDtypeStruct((NB, 2) + block, BF16),
    )(*sums)


def gathered(place, own, prev, parts):
    got = [turned_in_quad(part, -d) for d, part in enumerate(parts, 1)]
    own, prev, back = add_parts(place, own, prev, got)
    return [own, shifted(prev, -QUAD), shifted(back, -2 * QUAD)]


def swap(x):
    return lax.all_to_all(x, "head", split_axis=0, concat_axis=0, tiled=True)


def layer(query, key, value, output_gradient, pair_codes, pair_counts):
    y = lax.axis_index("blk") % QUAD
    place = jnp.full((1,), y, jnp.int32)
    codes, counts = pair_codes[0], pair_counts[0]
    keys = swap(pack_keys(key, value))
    packed = []
    for j in range(2):
        packed.append(pack_rows(j, query, output_gradient))
    own, prev, near, rows = [], [], [], []
    for j in range(2):
        own.append(keys[:, j])
        prev.append(shifted(own[j], QUAD))
        back = shifted(own[j], 2 * QUAD)
        sends = pack_window(place, own[j], prev[j], back)
        near.append([turned_in_quad(sends[d - 1], d) for d in range(1, QUAD)])
        rows.append(swap(packed[j]))
    filled, sums = None, []
    for j in range(2):
        both, own_sum, prev_sum, *parts = attend_call(codes, counts, place, rows[j], own[j], prev[j], near[j])
        got = swap(both)
        filled = unpack_rows(j, got, filled)
        sums += gathered(place, own_sum, prev_sum, parts)
    both = add_home(sums)
    got = swap(both)
    key_gradient, value_gradient = unpack_keys(got)
    return filled[0], filled[1], key_gradient, value_gradient


def solution(mesh):
    rows = P(("blk", "head"), None)
    return jax.shard_map(
        layer,
        mesh=mesh,
        in_specs=(rows, rows, rows, rows, P("blk", None, None), P("blk", None)),
        out_specs=(rows, rows, rows, rows),
        check_vma=False,
    )
```
